32 devices in a mesh: groups: 2 (over y), seq: 4 (over z), tensor: 4 (over x, core).
Axes of the slice: x: 2, y: 2, z: 4, core: 2. Of those that a mesh axis runs over, the one named last changes fastest.
Arguments:
- queries: bfloat16 [2048, 4096], P(('groups', 'seq'), 'tensor'), parts along dimension 0, may hold values from -6 to 6
- key_rows: bfloat16 [2048, 2048], P(('groups', 'seq'), 'tensor'), parts along dimension 0, may hold values from -6 to 6
- value_rows: bfloat16 [2048, 2048], P(('groups', 'seq'), 'tensor'), parts along dimension 0, may hold values from -6 to 6
- positions: int32 [2048], P(('groups', 'seq')), parts along dimension 0, may hold values from 0 to 131071, as said below
- residual: bfloat16 [2048, 3840], P(('groups', 'seq'), 'tensor'), parts along dimension 0, may hold values from -16 to 16
- direction: float32 [7680], P('groups'), parts along dimension 0, may hold values from -90 to 90
- out_weight: bfloat16 [4096, 3840], P('tensor'), may hold values from -0.375 to 0.375
Outputs:
- ablated: bfloat16 [2048, 3840], P(('groups', 'seq'), 'tensor'), parts along dimension 0
The draws below stay inside these ranges and needn't reach their ends.
There are 2 independent parts, one for each index of `groups`. The reference program is written for one: setup_inputs(seed, part) draws one part's arguments, and reference() takes and returns one part's arrays. A program takes and returns all parts, laid end to end along the dimension named above; an argument that names none is the same for every part. Nothing has to cross between parts.
Inputs may be any that keep to these rules, and one draw needn't show every extreme that they name: positions strictly increase along the slab, by at most 4 from one token to the next; the slab ends at the prompt's last position.
All inputs are finite; a program needn't handle non-finite values.
Results may differ from the reference program's by a relative error of at most 0.017.
Values may be sent and summed in bfloat16 or wider, within the bound.
No kernel may reach another device: no remote copies, remote signals or barrier semaphores. Data moves between devices by JAX's collectives and lax.ppermute only.
A program may use at most 64 MiB of HBM per device.

```python
import math
import jax
import jax.numpy as jnp
from jax import lax

D = 3840
HEADS = 16
KV_HEADS = 8
HD = 256
WINDOW = 1024
TOKENS = 1024
N_TENSOR = 4


def query_key_pair(key):
    pieces = jax.random.split(jax.random.fold_in(key, 11), 3)
    query_shape = (TOKENS, HEADS * HD)
    key_shape = (TOKENS, KV_HEADS * HD)
    query_vals = jnp.clip(2.0 * jax.random.normal(pieces[1], query_shape), -6.0, 6.0)
    key_vals = jnp.clip(jax.random.normal(pieces[2], key_shape), -6.0, 6.0)
    return (query_vals, key_vals)


def draw_queries(key, part):
    return query_key_pair(key)[0].astype(jnp.bfloat16)


def draw_key_rows(key, part):
    return query_key_pair(key)[1].astype(jnp.bfloat16)


def residual_direction_pair(key):
    pieces = jax.random.split(jax.random.fold_in(key, 23), 5)
    feature_ids = jnp.arange(D).astype(jnp.float32) / D
    jitter = jnp.exp(jax.random.uniform(pieces[1], (D,), minval=0.0, maxval=math.log(10.0)))
    ramp = 1.0 + 2.0 * feature_ids
    base_dir = jnp.clip(jax.random.normal(pieces[0], (D,)), -3.0, 3.0)
    noise_field = jnp.clip(jax.random.normal(pieces[4], (TOKENS, D)), -6.0, 6.0)
    raw_dir = base_dir * ramp * jitter
    magnitude = jnp.exp(jax.random.uniform(pieces[2], (TOKENS, 1), minval=math.log(5.0), maxval=math.log(60.0)))
    sign_col = jnp.where(jax.random.uniform(pieces[3], (TOKENS, 1)) < 0.5, -1.0, 1.0)
    resid_vals = noise_field + magnitude * sign_col * raw_dir[None, :] / 600.0
    return (resid_vals, raw_dir)


def draw_residual(key, part):
    return residual_direction_pair(key)[0].astype(jnp.bfloat16)


def draw_direction(key, part):
    return residual_direction_pair(key)[1].astype(jnp.float32)


def draw_positions(key, part):
    pieces = jax.random.split(jax.random.fold_in(key, 37), 2)
    rarely = (jax.random.randint(pieces[0], (TOKENS,), 0, 6) == 0).astype(jnp.int32)
    stride = 1 + rarely * jax.random.randint(pieces[1], (TOKENS,), 1, 4)
    after = jnp.cumsum(stride[::-1])[::-1] - stride
    return (131071 - after).astype(jnp.int32)


def shard_levels(own_key, dims, shards, least, high):
    def one(axis_at, shards_of):
        heights = jax.random.uniform(jax.random.fold_in(jax.random.fold_in(own_key, 6), axis_at), (shards_of,), jnp.float32, least / len(shards), high / len(shards))
        return jnp.repeat(jnp.exp(heights), dims[axis_at] // shards_of).reshape((-1,) + (1,) * (len(dims) - axis_at - 1))

    loudness = one(*shards[0])
    for cut in shards[1:]:
        loudness = loudness * one(*cut)
    return loudness


def bell_draw(key, extent, scale, bound, cuts=(), kind=jnp.bfloat16):
    factor_of = shard_levels(key, extent, cuts, -0.22, 0.18) if cuts else 1.0
    drawn = jax.random.normal(key, extent, jnp.float32) * scale * factor_of
    return jnp.minimum(jnp.maximum(drawn, -bound), bound).astype(kind)


def setup_inputs(seed: int = 0, part: int = 0) -> dict:
    seeds = jax.random.split(jax.random.key(seed), 8)
    own_keys = jax.random.split(jax.random.fold_in(seeds[7], part), 8)
    queries = draw_queries(jax.random.fold_in(jax.random.fold_in(seeds[7], part), 71), part)
    key_rows = draw_key_rows(jax.random.fold_in(jax.random.fold_in(seeds[7], part), 71), part)
    value_rows = bell_draw(own_keys[2], (TOKENS, KV_HEADS * HD), 1.0, 6.0, ((0, 4), (1, 4)))
    positions = draw_positions(jax.random.fold_in(jax.random.fold_in(seeds[7], part), 71), part)
    residual = draw_residual(jax.random.fold_in(jax.random.fold_in(seeds[7], part), 71), part)
    direction = draw_direction(jax.random.fold_in(jax.random.fold_in(seeds[7], part), 71), part)
    out_weight = bell_draw(seeds[6], (HEADS * HD, D), HD ** -0.5, 0.375, ((0, 4),))
    return {"queries": queries, "key_rows": key_rows, "value_rows": value_rows, "positions": positions, "residual": residual, "direction": direction, "out_weight": out_weight}


big_negative = -1e+30

def rotary_tables(positions, head_dim):
    half_dim = head_dim // 2
    freqs = jnp.power(10000.0, -jnp.arange(half_dim, dtype=jnp.float32) * 2.0 / head_dim)
    angles = positions.astype(jnp.float32)[:, None] * freqs[None, :]
    return (jnp.cos(angles)[:, None, :], jnp.sin(angles)[:, None, :])

def rotate_heads(block, cos_table, sin_table, head_dim):
    row_count = block.shape[0]
    head_count = block.shape[1] // head_dim
    half_dim = head_dim // 2
    widened = block.reshape(row_count, head_count, head_dim).astype(jnp.float32)
    first_half = widened[:, :, :half_dim]
    second_half = widened[:, :, half_dim:]
    turned = jnp.concatenate([first_half * cos_table - second_half * sin_table, second_half * cos_table + first_half * sin_table], axis=-1)
    return turned.reshape(row_count, head_count * head_dim)

def reference(queries, key_rows, value_rows, positions, residual, direction, out_weight):
    cos_table, sin_table = rotary_tables(positions, HD)
    rot_queries = (rotate_heads(queries, cos_table, sin_table, HD) * HD ** (-0.5)).astype(jnp.bfloat16)
    rot_keys = rotate_heads(key_rows, cos_table, sin_table, HD).astype(jnp.bfloat16)
    group_size = HEADS // KV_HEADS
    padding = jnp.zeros((WINDOW, KV_HEADS * HD), jnp.bfloat16)
    padded_keys = jnp.concatenate([padding, rot_keys], axis=0)
    padded_values = jnp.concatenate([padding, value_rows], axis=0)

    def attend(block_id):
        start = block_id * WINDOW
        query_part = lax.dynamic_slice_in_dim(rot_queries, start, WINDOW, 0).reshape(WINDOW, KV_HEADS, group_size, HD).astype(jnp.float32)
        key_part = lax.dynamic_slice_in_dim(padded_keys, start, 2 * WINDOW, 0).reshape(2 * WINDOW, KV_HEADS, HD).astype(jnp.float32)
        value_part = lax.dynamic_slice_in_dim(padded_values, start, 2 * WINDOW, 0).reshape(2 * WINDOW, KV_HEADS, HD).astype(jnp.float32)
        scores = jnp.einsum('qkgd,skd->kgqs', query_part, key_part)
        query_index = start + jnp.arange(WINDOW, dtype=jnp.int32)
        key_index = start - WINDOW + jnp.arange(2 * WINDOW, dtype=jnp.int32)
        gap_grid = query_index[:, None] - key_index[None, :]
        allowed = (gap_grid >= 0) & (gap_grid < WINDOW) & (key_index[None, :] >= 0)
        scores = jnp.where(allowed, scores, big_negative)
        row_max = lax.optimization_barrier(jnp.max(scores, axis=-1, keepdims=True))
        shifted = jnp.exp(scores - row_max)
        row_sum = lax.optimization_barrier(jnp.sum(shifted, axis=-1, keepdims=True))
        weights = (shifted / row_sum).astype(jnp.bfloat16)
        mixed = jnp.einsum('kgqs,skd->qkgd', weights.astype(jnp.float32), value_part)
        return mixed.astype(jnp.bfloat16).reshape(WINDOW, HEADS * HD)
    blocks = lax.map(attend, jnp.arange(TOKENS // WINDOW, dtype=jnp.int32))
    attended = blocks.reshape(TOKENS, HEADS * HD)
    rows_each = HEADS * HD // N_TENSOR
    attn_out = jnp.zeros((TOKENS, D), jnp.float32)
    for shard in range(N_TENSOR):
        piece = jnp.dot(attended[:, shard * rows_each:(shard + 1) * rows_each], out_weight[shard * rows_each:(shard + 1) * rows_each], preferred_element_type=jnp.float32)
        attn_out = attn_out + piece.astype(jnp.bfloat16).astype(jnp.float32)
    hidden_state = residual.astype(jnp.float32) + attn_out
    unit_dir = direction / jnp.sqrt(jnp.sum(direction * direction) + 1e-06)
    along = jnp.dot(hidden_state, unit_dir, precision=lax.Precision.HIGHEST)
    return (hidden_state - along[:, None] * unit_dir[None, :]).astype(jnp.bfloat16)
```

```python
import functools

import jax
import jax.numpy as jnp
from jax import lax
from jax.experimental import pallas as pl
from jax.experimental.pallas import tpu as pltpu
from jax.sharding import PartitionSpec as P

HD = 256
HALF = HD // 2
WINDOW = 1024
NEG = -1e30


def rotary_tables(positions):
    freqs = jnp.power(10000.0, -jnp.arange(HALF, dtype=jnp.float32) * 2.0 / HD)
    angles = positions.astype(jnp.float32)[:, None] * freqs[None, :]
    return jnp.cos(angles), jnp.sin(angles)


def rotate(ref, head, cos, sin, scale=None):
    first = ref[:, head * HD : head * HD + HALF].astype(jnp.float32)
    second = ref[:, head * HD + HALF : (head + 1) * HD].astype(jnp.float32)
    low = first * cos - second * sin
    high = second * cos + first * sin
    if scale is not None:
        low, high = low * scale, high * scale
    return low.astype(jnp.bfloat16), high.astype(jnp.bfloat16)


def pack_kernel(key_ref, value_ref, cos_ref, sin_ref, *out_refs, per):
    cos, sin = cos_ref[...], sin_ref[...]
    for chunk, out_ref in enumerate(out_refs):
        for place in range(per):
            head = chunk * per + place
            low, high = rotate(key_ref, head, cos, sin)
            out_ref[:, place * HD : place * HD + HALF] = low
            out_ref[:, place * HD + HALF : (place + 1) * HD] = high
            out_ref[:, (per + place) * HD : (per + place + 1) * HD] = value_ref[
                :, head * HD : (head + 1) * HD
            ]


def rotate_queries_kernel(query_ref, cos_ref, sin_ref, out_ref, *, heads):
    cos, sin = cos_ref[...], sin_ref[...]
    for head in range(heads):
        low, high = rotate(query_ref, head, cos, sin, HD ** (-0.5))
        out_ref[:, head * HD : head * HD + HALF] = low
        out_ref[:, head * HD + HALF : (head + 1) * HD] = high


def attend_kernel(*refs, distances, chunks, per, group, has_state, finish):
    refs = list(refs)
    place_ref = refs.pop(0)
    query_ref = refs.pop(0)
    blocks = [[refs.pop(0) for _ in range(chunks)] for _ in distances]
    state_in = (refs.pop(0), refs.pop(0)) if has_state else None
    rows = query_ref.shape[0]
    lane = lax.broadcasted_iota(jnp.int32, (group * rows, 128), 1)
    gap = lax.broadcasted_iota(jnp.int32, (rows, rows), 0) - lax.broadcasted_iota(
        jnp.int32, (rows, rows), 1
    )
    gap = jnp.concatenate([gap] * group, axis=0)
    for kv in range(chunks * per):
        chunk, place = divmod(kv, per)
        query = jnp.concatenate(
            [query_ref[:, (kv * group + g) * HD : (kv * group + g + 1) * HD] for g in range(group)],
            axis=0,
        )
        all_scores = []
        for block, distance in zip(blocks, distances):
            keys = block[chunk][:, place * HD : (place + 1) * HD]
            scores = lax.dot_general(
                query, keys, (((1,), (1,)), ((), ())), preferred_element_type=jnp.float32
            )
            if distance == 0:
                scores = jnp.where(gap >= 0, scores, NEG)
            else:
                if distance * rows + rows - 1 >= WINDOW:
                    scores = jnp.where(gap + distance * rows < WINDOW, scores, NEG)
                scores = scores + jnp.where(place_ref[0] >= distance, 0.0, NEG)
            all_scores.append(scores)
        peak = functools.reduce(jnp.maximum, all_scores)
        peak = jnp.max(peak, axis=-1, keepdims=True)
        if has_state:
            stats = state_in[1][kv]
            old_peak = stats[:, :1]
            old_sum = stats[:, 64:65]
            peak = jnp.maximum(peak, old_peak)
            shrink = jnp.exp(old_peak - peak)
        total = None
        mixed = None
        for block, scores in zip(blocks, all_scores):
            weights = jnp.exp(scores - peak)
            part = jnp.sum(weights, axis=-1, keepdims=True)
            values = block[chunk][:, (per + place) * HD : (per + place + 1) * HD]
            moved = jnp.dot(
                weights.astype(jnp.bfloat16), values, preferred_element_type=jnp.float32
            )
            total = part if total is None else total + part
            mixed = moved if mixed is None else mixed + moved
        if has_state:
            total = total + old_sum * shrink
            mixed = mixed + state_in[0][kv] * shrink
        if finish:
            out_ref = refs[0]
            done = (mixed / total).astype(jnp.bfloat16)
            for g in range(group):
                out_ref[:, (kv * group + g) * HD : (kv * group + g + 1) * HD] = done[
                    g * rows : (g + 1) * rows
                ]
        else:
            refs[0][kv] = mixed
            refs[1][kv] = jnp.where(lane < 64, peak, total)


def attend(place, queries, blocks, distances, state, finish, per, group):
    rows, width = queries.shape
    chunks = len(blocks[0])
    kv_heads = chunks * per
    vmem = pl.BlockSpec(memory_space=pltpu.VMEM)
    smem = pl.BlockSpec(memory_space=pltpu.SMEM)
    flat = [chunk for block in blocks for chunk in block]
    extra = list(state) if state is not None else []
    if finish:
        out_shape = jax.ShapeDtypeStruct((rows, width), jnp.bfloat16)
        out_specs = vmem
    else:
        out_shape = (
            jax.ShapeDtypeStruct((kv_heads, group * rows, HD), jnp.float32),
            jax.ShapeDtypeStruct((kv_heads, group * rows, 128), jnp.float32),
        )
        out_specs = (vmem, vmem)
    kernel = functools.partial(
        attend_kernel,
        distances=tuple(distances),
        chunks=chunks,
        per=per,
        group=group,
        has_state=state is not None,
        finish=finish,
    )
    return pl.pallas_call(
        kernel,
        out_shape=out_shape,
        in_specs=[smem] + [vmem] * (1 + len(flat) + len(extra)),
        out_specs=out_specs,
        name="attend_" + "_".join(str(d) for d in distances),
    )(place, queries, *flat, *extra)


def body(queries, key_rows, value_rows, positions, residual, direction, out_weight):
    rows = queries.shape[0]
    heads = queries.shape[1] // HD
    kv_heads = key_rows.shape[1] // HD
    group = heads // kv_heads
    seq_size = lax.axis_size("seq")
    tensor_size = lax.axis_size("tensor")
    seq_index = lax.axis_index("seq")
    tensor_index = lax.axis_index("tensor")
    hops = min(-(-(WINDOW - 1) // rows), seq_size - 1)
    chunks = 2 if kv_heads % 2 == 0 else 1
    per = kv_heads // chunks
    vmem = pl.BlockSpec(memory_space=pltpu.VMEM)

    cos, sin = rotary_tables(positions)
    own = pl.pallas_call(
        functools.partial(pack_kernel, per=per),
        out_shape=[jax.ShapeDtypeStruct((rows, 2 * per * HD), jnp.bfloat16)] * chunks,
        in_specs=[vmem] * 4,
        out_specs=[vmem] * chunks,
        name="pack",
    )(key_rows, value_rows, cos, sin)

    up = [(source, source + 1) for source in range(seq_size - 1)]
    blocks = [list(own)]
    for _ in range(hops):
        blocks.append([lax.ppermute(chunk, "seq", up) for chunk in blocks[-1]])

    rot_queries = pl.pallas_call(
        functools.partial(rotate_queries_kernel, heads=heads),
        out_shape=jax.ShapeDtypeStruct(queries.shape, jnp.bfloat16),
        in_specs=[vmem] * 3,
        out_specs=vmem,
        name="rotate_queries",
    )(queries, cos, sin)
    place = seq_index.astype(jnp.int32).reshape(1)
    state = None
    for distance in range(hops + 1):
        state = attend(
            place, rot_queries, [blocks[distance]], [distance], state, distance == hops, per, group
        )
    attended = state

    column_width = residual.shape[1]
    unit_dir = direction / jnp.sqrt(jnp.sum(direction * direction) + 1e-06)
    local_dir = lax.dynamic_slice_in_dim(unit_dir, tensor_index * column_width, column_width, 0)
    base_state = residual.astype(jnp.float32)
    weight_along = jnp.sum(out_weight.astype(jnp.float32) * unit_dir[None, :], axis=1)
    along = jnp.sum(base_state * local_dir[None, :], axis=1) + jnp.sum(
        attended.astype(jnp.float32) * weight_along[None, :], axis=1
    )

    pieces = {}
    for r in reversed(range(tensor_size)):
        columns = lax.dynamic_slice_in_dim(
            out_weight, (tensor_index ^ r) * column_width, column_width, 1
        )
        pieces[r] = jnp.dot(attended, columns, preferred_element_type=jnp.float32)
    bit = 1
    while bit < tensor_size:
        swap = [(device, device ^ bit) for device in range(tensor_size)]
        for r in reversed(range(tensor_size)):
            if r & bit and not r & (bit - 1):
                arrived = lax.ppermute(pieces[r].astype(jnp.bfloat16), "tensor", swap)
                pieces[r ^ bit] = pieces[r ^ bit] + arrived.astype(jnp.float32)
        bit *= 2
    along = lax.psum(along, "tensor")
    hidden_state = base_state + pieces[0]
    return (hidden_state - along[:, None] * local_dir[None, :]).astype(jnp.bfloat16)


def solution(mesh):
    return jax.shard_map(
        body,
        mesh=mesh,
        in_specs=(
            P(("groups", "seq"), "tensor"),
            P(("groups", "seq"), "tensor"),
            P(("groups", "seq"), "tensor"),
            P(("groups", "seq")),
            P(("groups", "seq"), "tensor"),
            P("groups"),
            P("tensor", None),
        ),
        out_specs=P(("groups", "seq"), "tensor"),
        check_vma=False,
    )
```

```python
import functools

import jax
import jax.numpy as jnp
from jax import lax
from jax.experimental import pallas as pl
from jax.experimental.pallas import tpu as pltpu
from jax.sharding import PartitionSpec as P

HD = 256
HALF = HD // 2
WINDOW = 1024
NEG = -1e30
F32 = jnp.float32
BF16 = jnp.bfloat16


def run(kernel, scalars, arrays, outs, name, scratch=()):
    smem = pl.BlockSpec(memory_space=pltpu.SMEM)
    vmem = pl.BlockSpec(memory_space=pltpu.VMEM)
    single = len(outs) == 1
    shapes = [pltpu.VMEM(shape, dtype) for shape, dtype in outs]
    return pl.pallas_call(
        kernel,
        out_shape=shapes[0] if single else shapes,
        in_specs=[smem] * len(scalars) + [vmem] * len(arrays),
        out_specs=vmem if single else [vmem] * len(outs),
        scratch_shapes=list(scratch),
        compiler_params=pltpu.CompilerParams(vmem_limit_bytes=24 * 2**20),
        name=name,
    )(*scalars, *[pltpu.with_memory_space_constraint(a, pltpu.VMEM) for a in arrays])


def after(value, *others):
    return lax.optimization_barrier((value, *others))[0]


def rotary_tables(positions):
    freqs = jnp.power(10000.0, -jnp.arange(HALF, dtype=F32) * 2.0 / HD)
    angles = positions.astype(F32)[:, None] * freqs[None, :]
    return jnp.cos(angles), jnp.sin(angles)


def rotate_kernel(ref, cos_ref, sin_ref, out_ref, *, scale):
    cos, sin = cos_ref[...], sin_ref[...]
    for head in range(ref.shape[1] // HD):
        first = ref[:, head * HD : head * HD + HALF].astype(F32)
        second = ref[:, head * HD + HALF : (head + 1) * HD].astype(F32)
        low = first * cos - second * sin
        high = second * cos + first * sin
        if scale is not None:
            low, high = low * scale, high * scale
        out_ref[:, head * HD : head * HD + HALF] = low.astype(BF16)
        out_ref[:, head * HD + HALF : (head + 1) * HD] = high.astype(BF16)


def rotate(block, cos, sin, scale, name):
    kernel = functools.partial(rotate_kernel, scale=scale)
    return run(kernel, (), (block, cos, sin), [(block.shape, BF16)], name)


def attend_kernel(*refs, distances, group, has_state, finish):
    refs = list(refs)
    place_ref = refs.pop(0)
    query_ref = refs.pop(0)
    blocks = [(refs.pop(0), refs.pop(0)) for _ in distances]
    state_in = (refs.pop(0), refs.pop(0)) if has_state else None
    rows = query_ref.shape[0]
    lane = lax.broadcasted_iota(jnp.int32, (group * rows, 128), 1)
    gap = lax.broadcasted_iota(jnp.int32, (rows, rows), 0) - lax.broadcasted_iota(
        jnp.int32, (rows, rows), 1
    )
    gap = jnp.concatenate([gap] * group, axis=0)
    for kv in range(query_ref.shape[1] // (group * HD)):
        mine = slice(kv * HD, (kv + 1) * HD)
        query = jnp.concatenate(
            [query_ref[:, (kv * group + g) * HD : (kv * group + g + 1) * HD] for g in range(group)],
            axis=0,
        )
        all_scores = []
        for (key_ref, _), distance in zip(blocks, distances):
            scores = lax.dot_general(
                query, key_ref[:, mine], (((1,), (1,)), ((), ())), preferred_element_type=F32
            )
            if distance == 0:
                scores = jnp.where(gap >= 0, scores, NEG)
            else:
                if distance * rows + rows - 1 >= WINDOW:
                    scores = jnp.where(gap + distance * rows < WINDOW, scores, NEG)
                scores = scores + jnp.where(place_ref[0] >= distance, 0.0, NEG)
            all_scores.append(scores)
        peak = functools.reduce(jnp.maximum, all_scores)
        peak = jnp.max(peak, axis=-1, keepdims=True)
        if has_state:
            stats = state_in[1][kv]
            old_peak = stats[:, :1]
            old_sum = stats[:, 64:65]
            peak = jnp.maximum(peak, old_peak)
            shrink = jnp.exp(old_peak - peak)
        total = None
        mixed = None
        for (_, value_ref), scores in zip(blocks, all_scores):
            weights = jnp.exp(scores - peak)
            part = jnp.sum(weights, axis=-1, keepdims=True)
            moved = jnp.dot(weights.astype(BF16), value_ref[:, mine], preferred_element_type=F32)
            total = part if total is None else total + part
            mixed = moved if mixed is None else mixed + moved
        if has_state:
            total = total + old_sum * shrink
            mixed = mixed + state_in[0][kv] * shrink
        if finish:
            done = (mixed / total).astype(BF16)
            for g in range(group):
                refs[0][:, (kv * group + g) * HD : (kv * group + g + 1) * HD] = done[
                    g * rows : (g + 1) * rows
                ]
        else:
            refs[0][kv] = mixed
            refs[1][kv] = jnp.where(lane < 64, peak, total)


def attend(place, queries, blocks, distances, state, finish, group):
    rows, width = queries.shape
    kv_heads = width // (group * HD)
    if finish:
        outs = [((rows, width), BF16)]
    else:
        outs = [((kv_heads, group * rows, HD), F32), ((kv_heads, group * rows, 128), F32)]
    kernel = functools.partial(
        attend_kernel,
        distances=tuple(distances),
        group=group,
        has_state=state is not None,
        finish=finish,
    )
    arrays = [queries, *[part for block in blocks for part in block], *(state or ())]
    return run(kernel, (place,), arrays, outs, "attend_" + "_".join(map(str, distances)))


def split3(value):
    high = value.astype(BF16)
    rest = value - high.astype(F32)
    middle = rest.astype(BF16)
    return high, middle, (rest - middle.astype(F32)).astype(BF16)


def terms8(value):
    rows = lax.broadcasted_iota(jnp.int32, (8, value.shape[1]), 0)
    high, middle, low = (term.astype(F32) for term in split3(value))
    return jnp.where(
        rows == 0, high, jnp.where(rows == 1, middle, jnp.where(rows == 2, low, 0.0))
    ).astype(BF16)


def add3(rows):
    return rows[0:1].astype(F32) + rows[1:2].astype(F32) + rows[2:3].astype(F32)


def direction_kernel(unit_ref, weight_ref, out_ref):
    product = lax.dot_general(
        terms8(unit_ref[...]),
        weight_ref[...],
        (((1,), (1,)), ((), ())),
        preferred_element_type=F32,
    )
    out_ref[...] = terms8(add3(product))


def residual_kernel(local_ref, residual_ref, out_ref):
    product = jnp.dot(terms8(local_ref[...]), residual_ref[...], preferred_element_type=F32)
    out_ref[...] = add3(product)


def project_kernel(*refs, width, with_along):
    refs = list(refs)
    where_ref, attended_ref, weight_ref = refs[:3]
    start = pl.multiple_of(where_ref[0], 128)
    half = 2 * width
    product = jnp.dot(
        attended_ref[...], weight_ref[:, pl.ds(start, half)], preferred_element_type=F32
    )
    if with_along:
        direction_ref, residual_ref, send_ref, keep_ref, along_ref, scratch = refs[3:]
    else:
        send_ref, keep_ref, scratch = refs[3:]
    scratch[...] = product.T
    keep_ref[...] = scratch[pl.ds(pl.multiple_of(where_ref[1], 8), width), :]
    send_ref[:width, :] = scratch[pl.ds(pl.multiple_of(where_ref[2], 8), width), :].astype(BF16)
    if with_along:
        along = residual_ref[...] + add3(
            lax.dot_general(
                direction_ref[...],
                attended_ref[...],
                (((1,), (1,)), ((), ())),
                preferred_element_type=F32,
            )
        )
        along_ref[...] = along
        send_ref[width:, :] = jnp.concatenate([terms8(along), jnp.zeros_like(terms8(along))], 0)


def pair_kernel(keep_ref, along_ref, came_ref, send_ref, along_out_ref):
    width = keep_ref.shape[0]
    send_ref[:width, :] = (keep_ref[...] + came_ref[:width, :].astype(F32)).astype(BF16)
    along = along_ref[...] + add3(came_ref[width : width + 8, :])
    along_out_ref[...] = along
    send_ref[width:, :] = jnp.concatenate([terms8(along), jnp.zeros_like(terms8(along))], 0)


def own_kernel(residual_ref, keep_ref, came_ref, out_ref):
    out_ref[...] = residual_ref[...].astype(F32) + keep_ref[...] + came_ref[...].astype(F32)


def final_kernel(own_ref, along_ref, came_ref, local_ref, out_ref):
    width = own_ref.shape[0]
    along = along_ref[...] + add3(came_ref[width : width + 8, :])
    hidden = own_ref[...] + came_ref[:width, :].astype(F32)
    out_ref[...] = (hidden - local_ref[...] * along).astype(BF16)


def unit_direction(direction):
    return direction / jnp.sqrt(jnp.sum(direction * direction) + 1e-06)


def local_part(unit, width):
    return lax.dynamic_slice_in_dim(unit, lax.axis_index("tensor") * width, width, 0)


def four_way_tail(attended, prepared, residual, out_weight):
    rows, width = residual.shape
    local_row, local_column, along_weight, residual_along = prepared
    tensor_index = lax.axis_index("tensor")
    core, chip = tensor_index % 2, tensor_index // 2
    far = jnp.stack([(1 - chip) * 2 * width, core * width, (1 - core) * width]).astype(jnp.int32)
    near = jnp.stack([chip * 2 * width, core * width, (1 - core) * width]).astype(jnp.int32)
    core_swap = [(0, 1), (1, 0), (2, 3), (3, 2)]
    chip_swap = [(0, 2), (2, 0), (1, 3), (3, 1)]
    scratch = [pltpu.VMEM((2 * width, rows), F32)]
    send, keep, along = run(
        functools.partial(project_kernel, width=width, with_along=True),
        (far,),
        (attended, out_weight, along_weight, residual_along),
        [((width + 16, rows), BF16), ((width, rows), F32), ((1, rows), F32)],
        "project_far",
        scratch,
    )
    came = lax.ppermute(send, "tensor", core_swap)
    send, along = run(
        pair_kernel,
        (),
        (keep, along, came),
        [((width + 16, rows), BF16), ((1, rows), F32)],
        "pair",
    )
    came_far = lax.ppermute(send, "tensor", chip_swap)
    send_near, keep_near = run(
        functools.partial(project_kernel, width=width, with_along=False),
        (near,),
        (after(attended, send), out_weight),
        [((width, rows), BF16), ((width, rows), F32)],
        "project_near",
        scratch,
    )
    came_near = lax.ppermute(send_near, "tensor", core_swap)
    own = run(
        own_kernel, (), (residual.T, keep_near, came_near), [((width, rows), F32)], "own"
    )
    out = run(
        final_kernel, (), (own, along, came_far, local_column), [((width, rows), BF16)], "final"
    )
    return out.T


def general_tail(attended, unit, residual, out_weight):
    width = residual.shape[1]
    tensor_size = lax.axis_size("tensor")
    tensor_index = lax.axis_index("tensor")
    local_dir = local_part(unit, width)
    base_state = residual.astype(F32)
    weight_along = jnp.sum(out_weight.astype(F32) * unit[None, :], axis=1)
    along = jnp.sum(base_state * local_dir[None, :], axis=1) + jnp.sum(
        attended.astype(F32) * weight_along[None, :], axis=1
    )
    pieces = {}
    for r in reversed(range(tensor_size)):
        columns = lax.dynamic_slice_in_dim(out_weight, (tensor_index ^ r) * width, width, 1)
        pieces[r] = jnp.dot(attended, columns, preferred_element_type=F32)
    bit = 1
    while bit < tensor_size:
        swap = [(device, device ^ bit) for device in range(tensor_size)]
        for r in reversed(range(tensor_size)):
            if r & bit and not r & (bit - 1):
                arrived = lax.ppermute(pieces[r].astype(BF16), "tensor", swap)
                pieces[r ^ bit] = pieces[r ^ bit] + arrived.astype(F32)
        bit *= 2
    along = lax.psum(along, "tensor")
    return (base_state + pieces[0] - along[:, None] * local_dir[None, :]).astype(BF16)


def body(queries, key_rows, value_rows, positions, residual, direction, out_weight):
    rows, width = residual.shape
    group = queries.shape[1] // key_rows.shape[1]
    seq_size = lax.axis_size("seq")
    tensor_size = lax.axis_size("tensor")
    hops = min(-(-(WINDOW - 1) // rows), seq_size - 1)
    four_way = tensor_size == 4 and width % 64 == 0
    place = lax.axis_index("seq").astype(jnp.int32).reshape(1)

    up = [(source, source + 1) for source in range(seq_size - 1)]
    values = [value_rows]
    keys = []
    cos, sin = rotary_tables(positions)
    keys.append(rotate(key_rows, cos, sin, None, "rotate_keys"))
    rot_queries = rotate(queries, cos, sin, HD ** (-0.5), "rotate_queries")
    state = None
    for distance in range(1, hops + 1):
        values.append(lax.ppermute(values[-1], "seq", up))
        last = keys[-1] if state is None else after(keys[-1], *state)
        keys.append(lax.ppermute(last, "seq", up))
        state = attend(
            place,
            rot_queries,
            [(keys[distance - 1], values[distance - 1])],
            [distance - 1],
            state,
            False,
            group,
        )

    unit = unit_direction(direction)
    if four_way:
        local = local_part(unit, width)
        prepared = (
            local.reshape(1, width),
            local.reshape(width, 1),
            run(direction_kernel, (), (unit.reshape(1, -1), out_weight), [((8, out_weight.shape[0]), BF16)], "direction"),
            run(residual_kernel, (), (local.reshape(1, width), residual.T), [((1, rows), F32)], "residual_along"),
        )
        *prepared, state0, state1 = lax.optimization_barrier((*prepared, *state))
        state = (state0, state1)
    attended = attend(
        place, rot_queries, [(keys[hops], values[hops])], [hops], state, True, group
    )
    if four_way:
        return four_way_tail(attended, prepared, residual, out_weight)
    return general_tail(attended, unit, residual, out_weight)


def solution(mesh):
    return jax.shard_map(
        body,
        mesh=mesh,
        in_specs=(
            P(("groups", "seq"), "tensor"),
            P(("groups", "seq"), "tensor"),
            P(("groups", "seq"), "tensor"),
            P(("groups", "seq")),
            P(("groups", "seq"), "tensor"),
            P("groups"),
            P("tensor", None),
        ),
        out_specs=P(("groups", "seq"), "tensor"),
        check_vma=False,
    )
```
